256 devices in a mesh: pairs: 64 (over z, x, core), win: 4 (over y).
Axes of the slice: x: 4, y: 4, z: 8, core: 2. Of those that a mesh axis runs over, the one named last changes fastest.
Arguments:
- raw_traces: bfloat16 [4, 320, 128, 512], P('win', None, 'pairs'), may hold values from -6 to 6
- tile_pairs: int32 [64, 4, 2], replicated, may hold values from -1 to 319, as said below
- block_slot: int32 [320], replicated, may hold values from 0 to 319, as said below
- win_offset: int32 [4], P('win'), may hold values from 0 to 128
Outputs:
- stacks: float32 [128, 256, 128, 128], P('win', 'pairs')
The draws below stay inside these ranges and needn't reach their ends.
Inputs may be any that keep to these rules, and one draw needn't show every extreme that they name: `tile_pairs`: row p lists owner p's tiles: pairs of block numbers, then rows of -1. Each owner has 1 to 4 tiles and some owner exactly 4. The blocks named in one owner's row are all different. `block_slot`: each slot holds exactly one block.
All inputs are finite; a program needn't handle non-finite values.
Results may differ from the reference program's by a relative error of at most 0.0041.
Values may be sent and summed in bfloat16 or wider, within the bound.
A program may use at most 192 MiB of HBM per device.

```python
import math
import jax
import jax.numpy as jnp
from jax import lax

CH = 128
NB_DEV = 5
SAMPLES = 256
LAGS = 128
TILES_DEV = 4
REC = 512
NBLK = 320
N_PAIRS = 64
N_WIN = 4


def layout_draw(key):
    block_total = NB_DEV * N_PAIRS
    block_slot = jax.random.permutation(jax.random.fold_in(key, 11), block_total).astype(jnp.int32)
    tile_tally = jax.random.randint(jax.random.fold_in(key, 12), (N_PAIRS,), 1, TILES_DEV + 1)
    fullest = jax.random.randint(jax.random.fold_in(key, 13), (), 0, N_PAIRS)
    tile_tally = jnp.where(jnp.arange(N_PAIRS) == fullest, TILES_DEV, tile_tally)
    owner_keys = jax.random.split(jax.random.fold_in(key, 14), N_PAIRS)

    def owner_blocks(owner_key):
        return jax.random.permutation(owner_key, block_total)[:2 * TILES_DEV]
    chosen = jax.vmap(owner_blocks)(owner_keys).reshape(N_PAIRS, TILES_DEV, 2)
    keep_mask = jnp.arange(TILES_DEV)[None, :] < tile_tally[:, None]
    tiles = jnp.where(keep_mask[:, :, None], chosen, -1)
    return (tiles.astype(jnp.int32), block_slot)


def draw_tile_pairs(key, part):
    return layout_draw(key)[0]


def draw_block_slot(key, part):
    return layout_draw(key)[1]


def place_ends(result, key, low, high):
    spot = [jax.random.randint(jax.random.fold_in(key, axis), (), 0, length) for axis, length in enumerate(result.shape)]
    main_axis = result.shape.index(max(result.shape))
    neighbour = spot[:main_axis] + [(spot[main_axis] + 1) % result.shape[main_axis]] + spot[main_axis + 1:]
    return result.at[tuple(spot)].set(low).at[tuple(neighbour)].set(high)


def steps_of(rng, extent, cuts, smallest, largest):
    gain, own = 1.0, jax.random.fold_in(rng, 6)
    for dim, shards_of in cuts:
        draws = jnp.exp(jax.random.uniform(jax.random.fold_in(own, dim), (shards_of,), jnp.float32, smallest / len(cuts), largest / len(cuts)))
        gain = gain * jnp.repeat(draws, extent[dim] // shards_of).reshape([-1 if axis == dim else 1 for axis in range(len(extent))])
    return gain


def noise(own_key, extent, scale, limit, cuts=(), kind=jnp.bfloat16):
    array = scale * jax.random.normal(own_key, extent, jnp.float32)
    if cuts:
        array = array * steps_of(own_key, extent, cuts, -0.22, 0.18)
    return jnp.clip(array, -limit, limit).astype(kind)


def setup_inputs(seed: int = 0) -> dict:
    key_of = jax.random.split(jax.random.key(seed), 5)
    return {
        "raw_traces": noise(key_of[0], (N_WIN, NBLK, CH, REC), 1.0, 6.0, ((0, 4), (2, 64))),
        "tile_pairs": draw_tile_pairs(jax.random.fold_in(key_of[4], 71), 0),
        "block_slot": draw_block_slot(jax.random.fold_in(key_of[4], 71), 0),
        "win_offset": place_ends(jax.random.randint(key_of[3], (N_WIN,), 0, LAGS + 1), jax.random.fold_in(key_of[3], 1), 0, LAGS).astype(jnp.int32),
    }


eps = 1e-06

def whiten(signal):
    length = signal.shape[-1]
    width = LAGS
    radius = LAGS // 2
    seg_count = length // width
    magnitude = jnp.abs(signal).reshape(signal.shape[:-1] + (seg_count, width))
    padded = jnp.pad(magnitude, [(0, 0)] * (magnitude.ndim - 2) + [(1, 1), (0, 0)])
    windows = jnp.concatenate([padded[..., :-2, :], padded[..., 1:-1, :], padded[..., 2:, :]], -1)
    rowpos = jnp.arange(3 * width)[:, None]
    colpos = jnp.arange(width)[None, :]
    band_matrix = (jnp.abs(rowpos - width - colpos) <= radius).astype(jnp.float32)
    totals = jnp.einsum('...ni,ij->...nj', windows, band_matrix, precision=lax.Precision.HIGHEST).reshape(signal.shape)
    position = jnp.arange(length)
    tally = (jnp.minimum(position, radius) + jnp.minimum(length - 1 - position, radius) + 1).astype(jnp.float32)
    return (signal / (totals / tally + eps)).astype(jnp.bfloat16)

def correlate(leading_blocks, trailing_blocks):
    seg_len = leading_blocks.shape[-1]
    samples = seg_len - LAGS
    half = LAGS // 2
    kernel = leading_blocks[..., half:half + samples].astype(jnp.float32)
    source = trailing_blocks[..., :seg_len - 1].astype(jnp.float32)
    source = jnp.transpose(source, (1, 0, 2))
    kernel = jnp.transpose(kernel, (1, 0, 2))
    return lax.conv_general_dilated(source, kernel, (1,), 'VALID', dimension_numbers=('NCH', 'OIH', 'CNH'), precision=lax.Precision.HIGHEST)

def reference(raw_traces, tile_pairs, block_slot, win_offset):
    seg_len = SAMPLES + LAGS

    def cut_window(record, offset):
        return lax.dynamic_slice_in_dim(record, offset, seg_len, 2)
    segments = jax.vmap(cut_window)(raw_traces.astype(jnp.float32), win_offset.astype(jnp.int32))
    whitened = whiten(segments)
    scale = 1.0 / math.sqrt(N_WIN * SAMPLES)
    flat_pairs = tile_pairs.reshape(-1, 2)

    def one_tile(pair):
        is_valid = pair[0] >= 0
        slot_first = block_slot[jnp.maximum(pair[0], 0)].astype(jnp.int32)
        slot_second = block_slot[jnp.maximum(pair[1], 0)].astype(jnp.int32)
        first_block = lax.dynamic_index_in_dim(whitened, slot_first, 1, keepdims=False)
        second_block = lax.dynamic_index_in_dim(whitened, slot_second, 1, keepdims=False)
        stack = correlate(first_block, second_block) * scale
        return jnp.where(is_valid, stack, jnp.zeros_like(stack))
    stacked = lax.map(one_tile, flat_pairs)
    return jnp.transpose(stacked, (1, 0, 2, 3))
```

```python
import math

import jax
import jax.numpy as jnp
from jax import lax
from jax.experimental import pallas as pl
from jax.experimental.pallas import tpu as pltpu
from jax.sharding import PartitionSpec as P

LAGS = 128
RADIUS = 64
SEG = 384
SAMPLES = 256
TILES = 4
NP = 64
NW = 4
ROWS = 32
SUB = 16
FULL = 60
BF = jnp.bfloat16
F32 = jnp.float32
MESH = pl.DeviceIdType.MESH
VMEM = pl.BlockSpec(memory_space=pltpu.VMEM)
SMEM = pl.BlockSpec(memory_space=pltpu.SMEM)
DMA = pltpu.SemaphoreType.DMA


def nt(a, b):
    return lax.dot_general(a, b, (((1,), (1,)), ((), ())), preferred_element_type=F32)


def prepare(raw, pairs, slots, offset, seconds, firsts):
    off = offset[0]
    rec = raw.shape[1]
    lanes = raw.shape[0]
    row = lax.broadcasted_iota(jnp.int32, (rec, SEG), 0) - off
    col = lax.broadcasted_iota(jnp.int32, (rec, SEG), 1)
    pick = (row == col).astype(BF)
    band = ((jnp.abs(row - col) <= RADIUS) & (row >= 0) & (row < SEG)).astype(BF)
    x = raw[...]
    segment = jnp.dot(x, pick, preferred_element_type=F32)
    totals = jnp.dot(jnp.abs(x), band, preferred_element_type=F32)
    at = lax.broadcasted_iota(jnp.int32, (1, SEG), 1)
    tally = (jnp.minimum(at, RADIUS) + jnp.minimum(SEG - 1 - at, RADIUS) + 1).astype(F32)
    white = (segment / (totals / tally + 1e-6)).astype(BF)

    slot = slots[...]
    parts = jnp.concatenate([slot // SUB, slot % SUB], 0).astype(F32).astype(BF)
    nblk = slot.shape[1]
    wanted = pairs[...]
    blk = lax.broadcasted_iota(jnp.int32, (2 * NP, nblk), 1)
    lane = lax.broadcasted_iota(jnp.int32, (2 * NP, lanes), 1)
    chan = lax.broadcasted_iota(jnp.int32, (2 * NP, 1), 0) % 2
    for k in range(TILES):
        for j in range(2):
            want = wanted[:, 2 * k + j : 2 * k + j + 1]
            found = nt((want == blk).astype(BF), parts)
            where = (SUB * found[:, 0:1] + found[:, 1:2]).astype(jnp.int32)
            source = jnp.where(want >= 0, 2 * where + chan, -1)
            rows = jnp.dot((source == lane).astype(BF), white, preferred_element_type=F32)
            if j:
                seconds[k] = rows.astype(BF)
            else:
                firsts[k] = rows[:, RADIUS : RADIUS + SAMPLES].astype(BF)


def prepare_kernel(raw, pairs, slots, offset, seconds, firsts):
    prepare(raw, pairs, slots, offset, seconds, firsts)


def exchange_kernel(out_s, out_f, got_s, got_f, send_s, recv_s, send_f, recv_f, send_y, recv_y, recv_y2):
    p = lax.axis_index("pairs")
    y = lax.axis_index("win")
    right, left, far = lax.rem(y + 1, NW), lax.rem(y + 3, NW), lax.rem(y + 2, NW)
    keeper = p // SUB
    barrier = pltpu.get_barrier_semaphore()

    def signal(q, w):
        pl.semaphore_signal(barrier, inc=1, device_id=(q, w), device_id_type=MESH)

    def greet(i, _):
        signal(lax.rem(p + i, NP), y)
        return 0

    lax.fori_loop(1, NP, greet, 0)
    signal(p, right)
    signal(p, left)

    def greet_first(i, _):
        q, w = SUB * y + lax.rem(i, SUB), i // SUB

        @pl.when(jnp.logical_not((q == p) & (w == y)))
        def _():
            signal(q, w)

        return 0

    lax.fori_loop(0, NP, greet_first, 0)
    pl.semaphore_wait(barrier, jnp.where(keeper == y, 2 * NP, 2 * NP + 1))

    mine = pl.ds(pl.multiple_of(2 * p, 2), 2)

    def pair_rows(q):
        return pl.ds(pl.multiple_of(2 * q, 2), 2)

    def wait(ref, sem):
        pltpu.make_async_copy(ref, ref, sem).wait()

    def send_tile(k):
        pltpu.make_async_copy(out_s.at[k, mine], got_s.at[y, k, mine], recv_s.at[k]).start()

        def one(i, _):
            q = lax.rem(p + lax.rem(i * 27, NP), NP)
            pltpu.make_async_remote_copy(
                src_ref=out_s.at[k, pair_rows(q)],
                dst_ref=got_s.at[y, k, mine],
                send_sem=send_s.at[jnp.maximum(i - FULL, 0)],
                recv_sem=recv_s.at[k],
                device_id=(q, y),
                device_id_type=MESH,
            ).start()
            return 0

        lax.fori_loop(1, NP, one, 0)

    kept = pl.ds(pl.multiple_of(2 * lax.rem(p, SUB), 2), 2)

    def send_first(q, sem):
        pltpu.make_async_remote_copy(
            src_ref=out_f.at[:, pair_rows(q)],
            dst_ref=got_f.at[y, :, kept],
            send_sem=send_f.at[sem],
            recv_sem=recv_f,
            device_id=(q, keeper),
            device_id_type=MESH,
        ).start()

    def send_firsts():
        def one(i, _):
            send_first(lax.rem(p + lax.rem(i * 27, NP), NP), jnp.maximum(i - FULL, 0))
            return 0

        lax.fori_loop(1, NP, one, 0)

        @pl.when(keeper == y)
        def _():
            pltpu.make_async_copy(out_f.at[:, mine], got_f.at[y, :, kept], recv_f).start()

        @pl.when(keeper != y)
        def _():
            send_first(p, NP - FULL)

    send_tile(0)
    send_firsts()
    for k in range(1, TILES):
        send_tile(k)

    half = got_s.shape[2] // 2

    def part(w, k, which=None):
        if which is None:
            return got_s.at[w, k]
        return got_s.at[w, k, pl.ds(which * half, half)]

    def pass_on(ref, send, recv, w):
        pltpu.make_async_remote_copy(
            src_ref=ref, dst_ref=ref, send_sem=send, recv_sem=recv, device_id=(p, w), device_id_type=MESH
        ).start()

    def first_step(k):
        wait(part(y, k), recv_s.at[k])
        pass_on(part(y, k), send_y.at[k, 0], recv_y.at[k, 0], right)
        pass_on(part(y, k), send_y.at[k, 1], recv_y.at[k, 1], left)

    def second_step(k):
        wait(part(left, k), recv_y.at[k, 0])
        pass_on(part(left, k, 0), send_y.at[k, 2], recv_y2.at[k, 0], right)
        wait(part(right, k), recv_y.at[k, 1])
        pass_on(part(right, k, 1), send_y.at[k, 3], recv_y2.at[k, 1], left)

    first_step(0)
    for k in range(1, TILES):
        first_step(k)
        second_step(k - 1)
    second_step(TILES - 1)
    for k in range(TILES):
        wait(part(far, k, 0), recv_y2.at[k, 0])
        wait(part(far, k, 1), recv_y2.at[k, 1])
    wait(got_f, recv_f)

    for out, sem in ((out_s, send_s), (out_f, send_f)):
        wait(out.at[:, pl.ds(0, 2 * FULL)], sem.at[0])
        for i in range(1, NP - FULL):
            wait(out.at[:, mine], sem.at[i])

    @pl.when(keeper != y)
    def _():
        wait(out_f.at[:, mine], send_f.at[NP - FULL])

    for k in range(TILES):
        wait(part(y, k), send_y.at[k, 0])
        wait(part(y, k), send_y.at[k, 1])
        wait(part(left, k, 0), send_y.at[k, 2])
        wait(part(right, k, 1), send_y.at[k, 3])


def correlate(second, first, wide, tall, flat):
    zeros = jnp.zeros((ROWS, LAGS), BF)
    for w in range(NW):
        tall[w] = second[w, 0].T
    for s in range(SUB):
        tails = []
        for w in range(NW):
            padded = jnp.concatenate([first[w, 0], zeros], 1)
            moved = pltpu.roll(padded, s, 1) if s else padded
            wide[pl.ds(s * ROWS, ROWS), pl.ds(w * SAMPLES, SAMPLES)] = moved[:, :SAMPLES]
            tail = moved[:, SAMPLES:]
            tails.append(pltpu.roll(tail, SUB * w, 1) if w else tail)
        wide[pl.ds(s * ROWS, ROWS), pl.ds(NW * SAMPLES, LAGS)] = tails[0] + tails[1] + tails[2] + tails[3]
    depth = NW * SAMPLES + NW * SUB
    for pair in range(LAGS // SUB // 2):
        sides = []
        for m in (2 * pair, 2 * pair + 1):
            pieces = [tall[w, pl.ds(SUB * m, SAMPLES)] for w in range(NW)]
            pieces += [tall[w, pl.ds(SUB * m + SAMPLES, SUB)] for w in range(NW)]
            sides.append(jnp.concatenate(pieces, 0))
        right = jnp.concatenate(sides, 1)
        both = jnp.dot(wide[:, :depth], right, preferred_element_type=F32)
        flat[2 * pair] = both[:, :LAGS]
        flat[2 * pair + 1] = both[:, LAGS:]


def correlate_kernel(second, first, out, wide, tall, flat):
    correlate(second, first, wide, tall, flat)
    scale = 1.0 / math.sqrt(NW * SAMPLES)

    def one(c, _):
        rows = [flat[m, pl.ds(c, SUB, stride=ROWS)] for m in range(LAGS // SUB)]
        out[c, 0] = (jnp.concatenate(rows, 0) * scale).T
        return 0

    lax.fori_loop(0, ROWS, one, 0, unroll=4)


def body(raw_traces, tile_pairs, block_slot, win_offset):
    nblk, local, rec = raw_traces.shape[1:]
    raw = raw_traces.reshape(nblk * local, rec)
    pairs = jnp.repeat(tile_pairs.reshape(NP, 2 * TILES), local, axis=0)
    seconds, firsts = pl.pallas_call(
        prepare_kernel,
        out_shape=[
            jax.ShapeDtypeStruct((TILES, 2 * NP, SEG), BF),
            jax.ShapeDtypeStruct((TILES, 2 * NP, SAMPLES), BF),
        ],
        in_specs=[VMEM, VMEM, VMEM, SMEM],
        out_specs=[VMEM, VMEM],
        name="prepare",
    )(raw, pairs, block_slot.reshape(1, nblk), win_offset)
    got_s, got_f = pl.pallas_call(
        exchange_kernel,
        out_shape=[
            jax.ShapeDtypeStruct((NW, TILES, 2 * NP, SEG), BF),
            jax.ShapeDtypeStruct((NW, TILES, ROWS, SAMPLES), BF),
        ],
        in_specs=[VMEM, VMEM],
        out_specs=[VMEM, VMEM],
        scratch_shapes=[
            DMA((NP - FULL,)),
            DMA((TILES,)),
            DMA((NP - FULL + 1,)),
            DMA,
            DMA((TILES, 4)),
            DMA((TILES, 2)),
            DMA((TILES, 2)),
        ],
        compiler_params=pltpu.CompilerParams(collective_id=0, has_side_effects=True),
        name="exchange",
    )(seconds, firsts)
    return pl.pallas_call(
        correlate_kernel,
        grid=(TILES,),
        out_shape=jax.ShapeDtypeStruct((ROWS, TILES, 2 * NP, LAGS), F32),
        in_specs=[
            pl.BlockSpec((NW, 1, 2 * NP, SEG), lambda k: (0, k, 0, 0)),
            pl.BlockSpec((NW, 1, ROWS, SAMPLES), lambda k: (0, k, 0, 0)),
        ],
        out_specs=pl.BlockSpec((ROWS, 1, 2 * NP, LAGS), lambda k: (0, k, 0, 0)),
        scratch_shapes=[
            pltpu.VMEM((SUB * ROWS, NW * SAMPLES + LAGS), BF),
            pltpu.VMEM((NW, SEG, 2 * NP), BF),
            pltpu.VMEM((LAGS // SUB, SUB * ROWS, LAGS), F32),
        ],
        compiler_params=pltpu.CompilerParams(vmem_limit_bytes=32 << 20),
        name="correlate",
    )(got_s, got_f)


def solution(mesh):
    return jax.shard_map(
        body,
        mesh=mesh,
        in_specs=(P("win", None, "pairs", None), P(), P(), P("win")),
        out_specs=P("win", "pairs", None, None),
        check_vma=False,
    )
```
